512 devices in a mesh: call: 64 (over z, y_hi, core), tensor: 8 (over x, y_lo).
Axes of the slice: x: 4, y: 4 (y_hi: 2, y_lo: 2; y = y_hi * 2 + y_lo), z: 16, core: 2. Of those that a mesh axis runs over, the one named last changes fastest.
Arguments:
- queries: bfloat16 [64, 768, 8192], P('call', None, 'tensor'), may hold values from -8 to 8
- child_kv: bfloat16 [64, 2, 768, 1024], P('call', None, None, 'tensor'), may hold values from -6 to 6
- summ_kv: bfloat16 [64, 2, 256, 1024], P('call', None, None, 'tensor'), may hold values from -6 to 6
- instr_pool: bfloat16 [64, 1024, 2, 1024], P('call', 'tensor'), may hold values from -16 to 16
- child_len: int32 [64], P('call'), may hold values from 256 to 768, as said below
- summ_len: int32 [64], P('call'), may hold values from 64 to 256, as said below
- owner_group: int32 [1], replicated, may hold values from 0 to 63
Outputs:
- attended: bfloat16 [64, 768, 8192], P('call', None, 'tensor')
The draws below stay inside these ranges and needn't reach their ends.
Inputs may be any that keep to these rules, and one draw needn't show every extreme that they name: `child_len`: one call has exactly 768 child tokens and one exactly 256. `summ_len`: one call has exactly 256 summary tokens and one exactly 64.
All inputs are finite; a program needn't handle non-finite values.
Results may differ from the reference program's by a relative error of at most 0.006.
Values may be sent and summed in bfloat16 or wider, within the bound.
A program may use at most 64 MiB of HBM per device.

```python
import math
import jax
import jax.numpy as jnp
from jax import lax

QH = 64
KVH = 8
HD = 128
CAP = 768
SUMM = 256
INSTR = 1024
CALLS = 64


def draw_queries(key, part):
    first = jax.random.fold_in(jax.random.fold_in(key, 11), 0)
    shape = (CALLS, CAP, QH * HD)
    base = jnp.clip(jax.random.normal(first, shape, jnp.float32), -6.0, 6.0)
    return base.astype(jnp.bfloat16)


def draw_instr_pool(key, part):
    first = jax.random.fold_in(jax.random.fold_in(key, 23), 0)
    shape = (CALLS, INSTR, 2, KVH * HD)
    base = jnp.clip(jax.random.normal(first, shape, jnp.float32), -6.0, 6.0)
    return base.astype(jnp.bfloat16)


def ragged_counts(key, lowest, highest):
    first, second, third = jax.random.split(key, 3)
    counts = jax.random.randint(first, (CALLS,), lowest, highest + 1, dtype=jnp.int32)
    top_at = jax.random.randint(second, (), 0, CALLS, dtype=jnp.int32)
    low_at = (top_at + 1 + jax.random.randint(third, (), 0, CALLS - 1, dtype=jnp.int32)) % CALLS
    counts = counts.at[top_at].set(highest)
    return counts.at[low_at].set(lowest)


def draw_child_len(key, part):
    return ragged_counts(jax.random.fold_in(key, 37), CAP // 3, CAP)


def draw_summ_len(key, part):
    return ragged_counts(jax.random.fold_in(key, 41), SUMM // 4, SUMM)


def level_of(key, shape, pieces, low, high):
    gain, own = 1.0, jax.random.fold_in(key, 6)
    for position, shards_of in pieces:
        steps = jnp.exp(jax.random.uniform(jax.random.fold_in(own, position), (shards_of,), jnp.float32, low / len(pieces), high / len(pieces)))
        gain = gain * jnp.repeat(steps, shape[position] // shards_of).reshape([-1 if axis == position else 1 for axis in range(len(shape))])
    return gain


def centred(rng, extent, scale, bound, shards=(), held_as=jnp.bfloat16):
    entries = scale * jax.random.normal(rng, extent, jnp.float32)
    if shards:
        entries = entries * level_of(rng, extent, shards, -0.22, 0.18)
    return jnp.clip(entries, -bound, bound).astype(held_as)


def setup_inputs(seed: int = 0) -> dict:
    streams_of = jax.random.split(jax.random.key(seed), 8)
    queries = draw_queries(jax.random.fold_in(streams_of[7], 71), 0)
    child_kv = centred(streams_of[1], (CALLS, 2, CAP, KVH * HD), 1.0, 6.0, ((0, 64), (3, 8)))
    summ_kv = centred(streams_of[2], (CALLS, 2, SUMM, KVH * HD), 1.0, 6.0, ((0, 64), (3, 8)))
    instr_pool = draw_instr_pool(jax.random.fold_in(streams_of[7], 71), 0)
    child_len = draw_child_len(jax.random.fold_in(streams_of[7], 71), 0)
    summ_len = draw_summ_len(jax.random.fold_in(streams_of[7], 71), 0)
    owner_group = jax.random.randint(streams_of[6], (1,), 0, CALLS).astype(jnp.int32)
    return dict(queries=queries, child_kv=child_kv, summ_kv=summ_kv, instr_pool=instr_pool, child_len=child_len, summ_len=summ_len, owner_group=owner_group)


NEG = -1e+30

def head_split(packed, heads):
    total = packed.shape[0]
    width = packed.shape[1]
    return packed.reshape(total, heads, width // heads).transpose(1, 0, 2)

def partial_softmax(query_head, key_rows, value_rows, allowed):
    score_scale = 1.0 / math.sqrt(query_head.shape[1])
    scores = lax.dot_general(query_head, key_rows, (((1,), (1,)), ((), ())), preferred_element_type=jnp.float32) * score_scale
    scores = jnp.where(allowed, scores, NEG)
    maxima = lax.optimization_barrier(jnp.max(scores, axis=1, keepdims=True))
    expons = jnp.where(allowed, jnp.exp(scores - maxima), 0.0)
    totals = lax.optimization_barrier(jnp.sum(expons, axis=1, keepdims=True))
    weights = expons.astype(jnp.bfloat16)
    return (maxima, totals, jnp.dot(weights, value_rows, preferred_element_type=jnp.float32))

def over_heads(query_heads, key_heads, value_heads, allowed):
    group = query_heads.shape[0] // key_heads.shape[0]

    def single(pair):
        query_head, number = pair
        key_rows = lax.dynamic_index_in_dim(key_heads, number // group, 0, keepdims=False)
        value_rows = lax.dynamic_index_in_dim(value_heads, number // group, 0, keepdims=False)
        return partial_softmax(query_head, key_rows, value_rows, allowed)
    return lax.map(single, (query_heads, jnp.arange(query_heads.shape[0], dtype=jnp.int32)))

def reference(queries, child_kv, summ_kv, instr_pool, child_len, summ_len, owner_group):
    instr_rows = lax.dynamic_index_in_dim(instr_pool, owner_group[0], 0, keepdims=False)
    prev_kv = jnp.concatenate([jnp.zeros_like(summ_kv[:1]), summ_kv[:-1]], 0)
    prev_len = jnp.concatenate([jnp.zeros((1,), jnp.int32), summ_len[:-1].astype(jnp.int32)], 0)

    def per_call(items):
        query_mat, own_kv, sib_kv, sib_len, own_len = items
        length = query_mat.shape[0]
        heads = query_mat.shape[1] // HD
        kv_heads = own_kv.shape[2] // HD
        positions = jnp.arange(length, dtype=jnp.int32)
        allowed = jnp.concatenate([jnp.ones((length, INSTR), bool), jnp.broadcast_to(jnp.arange(SUMM, dtype=jnp.int32)[None, :] < sib_len, (length, SUMM)), positions[None, :] <= positions[:, None]], 1)
        key_all = jnp.concatenate([instr_rows[:, 0], sib_kv[0], own_kv[0]], 0)
        value_all = jnp.concatenate([instr_rows[:, 1], sib_kv[1], own_kv[1]], 0)
        maxima, totals, sums = over_heads(head_split(query_mat, heads), head_split(key_all, kv_heads), head_split(value_all, kv_heads), allowed)
        result = (sums / totals).transpose(1, 0, 2).reshape(length, heads * HD)
        result = jnp.where((positions < own_len)[:, None], result, 0.0)
        return result.astype(jnp.bfloat16)
    return lax.map(per_call, (queries, child_kv, prev_kv, prev_len, child_len.astype(jnp.int32)))
```

```python
import functools
import math

import jax
import jax.numpy as jnp
from jax import lax
from jax.experimental import pallas as pl
from jax.experimental.pallas import tpu as pltpu
from jax.sharding import PartitionSpec as P

HD = 128
NEG = -1e30
LOG2E = 1.4426950408889634
MESH = pl.DeviceIdType.MESH
QT = 256


def ring_offset(j, n):
    odd = j % 2
    return odd * ((j + 1) // 2) + (1 - odd) * (n - j // 2)


def kernel(
    dims,
    owner_ref, clen_ref, q_ref, ckv_ref, skv_ref, slen_ref, pool_ref,
    out_ref,
    r1, x2, r2, x3, instr, prev, plen, m_ref, l_ref, acc_ref,
    s1, v1, s2, v2, s3, v3, sy, vy, sk, vk, sp, vp,
):
    nz, ns, nt = dims
    c = lax.axis_index("call")
    t = lax.axis_index("tensor")
    z = c // ns
    s = c % ns
    ncall = nz * ns
    plane = ns * nt
    me = s * nt + t
    heads = q_ref.shape[1] // HD
    rows = q_ref.shape[0]
    nq = rows // QT
    scale2 = LOG2E / math.sqrt(HD)

    def plane_dev(p):
        return (z * ns + p // nt, p % nt)

    def rcopy(src, dst, ssem, rsem, dev):
        return pltpu.make_async_remote_copy(
            src_ref=src, dst_ref=dst, send_sem=ssem, recv_sem=rsem,
            device_id=dev, device_id_type=MESH,
        )

    barrier = pltpu.get_barrier_semaphore()

    @pl.loop(1, plane)
    def _(j):
        pl.semaphore_signal(barrier, inc=1, device_id=plane_dev((me + j) % plane), device_id_type=MESH)

    @pl.loop(1, nz)
    def _(j):
        pl.semaphore_signal(
            barrier, inc=1, device_id=(((z + j) % nz) * ns + s, t), device_id_type=MESH
        )

    nxt = ((c + 1) % ncall, t)
    prv = ((c + ncall - 1) % ncall, t)
    pl.semaphore_signal(barrier, inc=1, device_id=nxt, device_id_type=MESH)
    pl.semaphore_signal(barrier, inc=1, device_id=prv, device_id_type=MESH)

    def own_part(h):
        col = pl.multiple_of(h * HD, HD)
        for i in range(nq):
            n = (i + 1) * QT
            rs = slice(i * QT, (i + 1) * QT)
            q = q_ref[rs, pl.ds(col, HD)]
            k = ckv_ref[0, 0:n, :]
            v = ckv_ref[1, 0:n, :]
            sc = lax.dot_general(q, k, (((1,), (1,)), ((), ())), preferred_element_type=jnp.float32)
            r = lax.broadcasted_iota(jnp.int32, (QT, QT), 0)
            cc = lax.broadcasted_iota(jnp.int32, (QT, QT), 1)
            diag = jnp.where(cc <= r, sc[:, n - QT : n], NEG)
            if i > 0:
                sc = jnp.concatenate([sc[:, 0 : n - QT], diag], axis=1)
            else:
                sc = diag
            m = jnp.max(sc, axis=1, keepdims=True)
            p = jnp.exp2((sc - m) * scale2)
            l = jnp.sum(p, axis=1, keepdims=True)
            acc = jnp.dot(p.astype(jnp.bfloat16), v, preferred_element_type=jnp.float32)
            m_ref[h, rs, :] = jnp.broadcast_to(m, (QT, HD))
            l_ref[h, rs, :] = jnp.broadcast_to(l, (QT, HD))
            acc_ref[h, rs, :] = acc

    def merge(h, i, sc, v):
        rs = slice(i * QT, (i + 1) * QT)
        m0 = m_ref[h, rs, :][:, 0:1]
        m = jnp.maximum(m0, jnp.max(sc, axis=1, keepdims=True))
        p = jnp.exp2((sc - m) * scale2)
        a = jnp.exp2((m0 - m) * scale2)
        l = l_ref[h, rs, :][:, 0:1] * a + jnp.sum(p, axis=1, keepdims=True)
        acc = acc_ref[h, rs, :] * a + jnp.dot(
            p.astype(jnp.bfloat16), v, preferred_element_type=jnp.float32
        )
        return m, l, acc

    def prev_part(h):
        col = pl.multiple_of(h * HD, HD)
        ns_ = prev.shape[1]
        ln = jnp.where(c > 0, plen[0:1, 0:1], 0)
        bias = jnp.where(lax.broadcasted_iota(jnp.int32, (1, ns_), 1) < ln, 0.0, NEG)
        for i in range(nq):
            rs = slice(i * QT, (i + 1) * QT)
            q = q_ref[rs, pl.ds(col, HD)]
            sc = lax.dot_general(
                q, prev[0], (((1,), (1,)), ((), ())), preferred_element_type=jnp.float32
            )
            m, l, acc = merge(h, i, jnp.where(bias < -1.0, NEG, sc), prev[1])
            m_ref[h, rs, :] = jnp.broadcast_to(m, (QT, HD))
            l_ref[h, rs, :] = jnp.broadcast_to(l, (QT, HD))
            acc_ref[h, rs, :] = acc

    def instr_part(h):
        col = pl.multiple_of(h * HD, HD)
        count = ns * nz * instr.shape[3]
        k = instr[:, :, 0].reshape(count, HD)
        v = instr[:, :, 1].reshape(count, HD)
        for i in range(nq):
            rs = slice(i * QT, (i + 1) * QT)
            q = q_ref[rs, pl.ds(col, HD)]
            sc = lax.dot_general(q, k, (((1,), (1,)), ((), ())), preferred_element_type=jnp.float32)
            m, l, acc = merge(h, i, sc, v)
            pos = lax.broadcasted_iota(jnp.int32, (QT, HD), 0) + i * QT
            res = jnp.where(pos < clen_ref[0], acc / l, 0.0)
            out_ref[rs, pl.ds(col, HD)] = res.astype(jnp.bfloat16)

    pl.semaphore_wait(barrier, plane - 1 + nz - 1 + 2)

    def p1(j):
        dst = (me + j) % plane
        return rcopy(
            pool_ref.at[dst % nt, dst // nt], r1.at[s, t], s1.at[j], v1.at[j], plane_dev(dst)
        )

    def p1_in(j):
        src = (me + plane - j) % plane
        return rcopy(
            pool_ref.at[0, 0], r1.at[src // nt, src % nt], s1.at[j], v1.at[j], plane_dev(src)
        )

    @pl.loop(1, plane)
    def _(j):
        p1(j).start()

    pk = rcopy(skv_ref, prev, sp.at[0], vp.at[0], nxt)
    pn = rcopy(slen_ref, plen, sp.at[1], vp.at[1], nxt)
    pk.start()
    pn.start()
    r1[s, t] = pool_ref[t, s]

    @pl.loop(0, heads)
    def _(h):
        own_part(h)

    @pl.loop(1, plane)
    def _(j):
        p1_in(j).wait_recv()

    owner = owner_ref[0]
    owner_s = owner % ns
    owner_z = owner // ns
    for b in range(nt):
        for f in range(nz // nt):
            per = x2.shape[2]
            x2[b * (nz // nt) + f] = r1[owner_s, b, :, f * per : (f + 1) * per, :]

    def p2(j):
        o = (z + ring_offset(j, nz)) % nz
        return rcopy(x2.at[o], r2.at[z], s2.at[j], v2.at[j], (o * ns + s, t))

    def p2_in(j):
        o = (z + nz - ring_offset(j, nz)) % nz
        return rcopy(x2.at[0], r2.at[o], s2.at[j], v2.at[j], (o * ns + s, t))

    @pl.loop(1, nz)
    def _(j):
        p2(j).start()

    r2[z] = x2[z]
    pk.wait_recv()
    pn.wait_recv()

    @pl.loop(0, heads)
    def _(h):
        prev_part(h)

    @pl.loop(1, nz)
    def _(j):
        p2_in(j).wait_recv()

    share = r2[owner_z]
    x3[...] = share
    instr[s, z] = share

    def p3(j):
        o = (z + ring_offset(j, nz)) % nz
        return rcopy(x3, instr.at[s, z], s3.at[j], v3.at[j], (o * ns + s, t))

    def p3_in(j):
        o = (z + nz - ring_offset(j, nz)) % nz
        return rcopy(x3, instr.at[s, o], s3.at[j], v3.at[j], (o * ns + s, t))

    @pl.loop(1, nz)
    def _(j):
        p3(j).start()

    sh = ns // 2
    mate_k = (z * ns + (s // 2) * 2 + 1 - s % 2, t)
    mate_y = (z * ns + (s + sh) % ns, t)
    s_k = (s // 2) * 2 + 1 - s % 2
    s_y = (s + sh) % ns
    s_d = (s_k + sh) % ns

    def slot(j):
        return (z + nz - ring_offset(j, nz)) % nz

    def to_y(j):
        return rcopy(instr.at[s, slot(j)], instr.at[s, slot(j)], sy.at[j], vy.at[j], mate_y)

    def from_y(j):
        return rcopy(instr.at[s_y, slot(j)], instr.at[s_y, slot(j)], sy.at[j], vy.at[j], mate_y)

    def to_k(a, w, j):
        return rcopy(instr.at[a, slot(j)], instr.at[a, slot(j)], sk.at[w, j], vk.at[w, j], mate_k)

    to_y(0).start()
    to_k(s, 0, 0).start()

    @pl.loop(1, nz)
    def _(j):
        p3_in(j).wait_recv()
        to_y(j).start()
        to_k(s, 0, j).start()

    @pl.loop(0, nz)
    def _(j):
        from_y(j).wait_recv()
        to_k(s_y, 1, j).start()

    @pl.loop(0, nz)
    def _(j):
        to_k(s_k, 0, j).wait_recv()
        to_k(s_d, 1, j).wait_recv()

    @pl.loop(0, heads)
    def _(h):
        instr_part(h)

    @pl.loop(1, plane)
    def _(j):
        p1(j).wait_send()

    pk.wait_send()
    pn.wait_send()

    @pl.loop(1, nz)
    def _(j):
        p2(j).wait_send()
        p3(j).wait_send()

    @pl.loop(0, nz)
    def _(j):
        to_y(j).wait_send()
        to_k(s, 0, j).wait_send()
        to_k(s_y, 1, j).wait_send()


def shards(dims, queries, child_kv, summ_kv, instr_pool, child_len, summ_len, owner_group):
    nz, ns, nt = dims
    rows, width = queries.shape[1], queries.shape[2]
    heads = width // HD
    block = instr_pool.shape[1]
    summ = summ_kv.shape[2]
    quarter = block // ns
    pool = instr_pool[0].reshape(ns, quarter, 2, nt, HD).transpose(3, 0, 2, 1, 4)
    slen = jnp.broadcast_to(summ_len[0], (8, 128)).astype(jnp.int32)
    piece = quarter * nt // nz
    vm = pl.BlockSpec(memory_space=pltpu.VMEM)
    sm = pl.BlockSpec(memory_space=pltpu.SMEM)
    bf = jnp.bfloat16
    dma = pltpu.SemaphoreType.DMA
    out = pl.pallas_call(
        functools.partial(kernel, dims),
        name="merge_attention",
        out_shape=jax.ShapeDtypeStruct((rows, width), bf),
        in_specs=[sm, sm, vm, vm, vm, vm, vm],
        out_specs=vm,
        scratch_shapes=[
            pltpu.VMEM((ns, nt, 2, quarter, HD), bf),
            pltpu.VMEM((nz, 2, piece, HD), bf),
            pltpu.VMEM((nz, 2, piece, HD), bf),
            pltpu.VMEM((2, piece, HD), bf),
            pltpu.VMEM((ns, nz, 2, piece, HD), bf),
            pltpu.VMEM((2, summ, HD), bf),
            pltpu.VMEM((8, 128), jnp.int32),
            pltpu.VMEM((heads, rows, HD), jnp.float32),
            pltpu.VMEM((heads, rows, HD), jnp.float32),
            pltpu.VMEM((heads, rows, HD), jnp.float32),
            dma((ns * nt,)), dma((ns * nt,)),
            dma((nz,)), dma((nz,)),
            dma((nz,)), dma((nz,)),
            dma((nz,)), dma((nz,)),
            dma((2, nz)), dma((2, nz)),
            dma((2,)), dma((2,)),
        ],
        compiler_params=pltpu.CompilerParams(
            collective_id=0, has_side_effects=True, vmem_limit_bytes=56 * 1024 * 1024
        ),
    )(owner_group, child_len, queries[0], child_kv[0], summ_kv[0], slen, pool)
    return out[None]


def solution(mesh):
    sizes = dict(mesh.shape)
    ns = 4
    dims = (sizes["call"] // ns, ns, sizes["tensor"])
    in_specs = (
        P("call", None, "tensor"),
        P("call", None, None, "tensor"),
        P("call", None, None, "tensor"),
        P("call", "tensor", None, None),
        P("call"),
        P("call"),
        P(),
    )
    out_specs = P("call", None, "tensor")
    return jax.shard_map(
        functools.partial(shards, dims), mesh=mesh, in_specs=in_specs, out_specs=out_specs, check_vma=False
    )
```

```python
import functools
import math

import jax
import jax.numpy as jnp
from jax import lax
from jax.experimental import pallas as pl
from jax.experimental.pallas import tpu as pltpu
from jax.sharding import PartitionSpec as P

HD = 128
NEG = -1e30
LOG2E = 1.4426950408889634
MESH = pl.DeviceIdType.MESH
QT = 256


def ring_offset(j, n):
    odd = j % 2
    return odd * ((j + 1) // 2) + (1 - odd) * (n - j // 2)


def kernel(
    dims,
    owner_ref, clen_ref, q_ref, ckv_ref, skv_ref, slen_ref, pool_ref,
    out_ref,
    r1, x2, r2, x3, instr, prev, plen, mlen, m_ref, acc_ref,
    s1, v1, s2, v2, s3, v3, sy, vy, sk, vk, sp, vp,
):
    nz, ns, nt = dims
    c = lax.axis_index("call")
    t = lax.axis_index("tensor")
    z = c // ns
    s = c % ns
    ncall = nz * ns
    plane = ns * nt
    me = s * nt + t
    heads = q_ref.shape[1] // HD
    rows = q_ref.shape[0]
    nq = rows // QT
    scale2 = LOG2E / math.sqrt(HD)

    def plane_dev(p):
        return (z * ns + p // nt, p % nt)

    def rcopy(src, dst, ssem, rsem, dev):
        return pltpu.make_async_remote_copy(
            src_ref=src, dst_ref=dst, send_sem=ssem, recv_sem=rsem,
            device_id=dev, device_id_type=MESH,
        )

    barrier = pltpu.get_barrier_semaphore()

    @pl.loop(1, plane)
    def _(j):
        pl.semaphore_signal(barrier, inc=1, device_id=plane_dev((me + j) % plane), device_id_type=MESH)

    @pl.loop(1, nz)
    def _(j):
        pl.semaphore_signal(
            barrier, inc=1, device_id=(((z + j) % nz) * ns + s, t), device_id_type=MESH
        )

    nxt = ((c + 1) % ncall, t)
    prv = ((c + ncall - 1) % ncall, t)
    pl.semaphore_signal(barrier, inc=1, device_id=nxt, device_id_type=MESH)
    pl.semaphore_signal(barrier, inc=1, device_id=prv, device_id_type=MESH)

    def dot_t(a, b):
        return lax.dot_general(a, b, (((1,), (1,)), ((), ())), preferred_element_type=jnp.float32)

    def with_ones(v):
        return jnp.concatenate([v, jnp.ones_like(v)], axis=1)

    def wide(m, n):
        return jnp.concatenate([m] * (n // HD), axis=1)

    def row_max(sc):
        return jnp.broadcast_to(jnp.max(sc, axis=1, keepdims=True), (QT, HD))

    def weights(sc, m):
        return jnp.exp2((sc - wide(m, sc.shape[1])) * scale2).astype(jnp.bfloat16)

    def rows_of(i):
        return slice(i * QT, (i + 1) * QT)

    def q_tile(h, i):
        return q_ref[rows_of(i), pl.ds(pl.multiple_of(h * HD, HD), HD)]

    def own_part(h):
        r = lax.broadcasted_iota(jnp.int32, (QT, QT), 0)
        cc = lax.broadcasted_iota(jnp.int32, (QT, QT), 1)
        for i in range(nq):
            n = (i + 1) * QT
            sc = dot_t(q_tile(h, i), ckv_ref[0, 0:n, :])
            diag = jnp.where(cc <= r, sc[:, n - QT : n], NEG)
            if i > 0:
                sc = jnp.concatenate([sc[:, 0 : n - QT], diag], axis=1)
            else:
                sc = diag
            m = row_max(sc)
            m_ref[h, rows_of(i), :] = m
            acc_ref[h, rows_of(i), :] = jnp.dot(
                weights(sc, m), with_ones(ckv_ref[1, 0:n, :]), preferred_element_type=jnp.float32
            )

    def merge(h, i, sc, v2):
        m0 = m_ref[h, rows_of(i), :]
        m = jnp.maximum(m0, row_max(sc))
        a = jnp.exp2((m0 - m) * scale2)
        acc = acc_ref[h, rows_of(i), :] * wide(a, 2 * HD) + jnp.dot(
            weights(sc, m), v2, preferred_element_type=jnp.float32
        )
        return m, acc

    def prev_part(h):
        count = prev.shape[1]
        ln = jnp.where(c > 0, plen[0:1, 0:1], 0)
        ok = jnp.broadcast_to(
            lax.broadcasted_iota(jnp.int32, (1, count), 1) < ln, (QT, count)
        )
        v2 = with_ones(prev[1])
        for i in range(nq):
            sc = jnp.where(ok, dot_t(q_tile(h, i), prev[0]), NEG)
            m, acc = merge(h, i, sc, v2)
            m_ref[h, rows_of(i), :] = m
            acc_ref[h, rows_of(i), :] = acc

    def instr_part(h, qa, qb, last):
        count = nz * instr.shape[3]
        k = jnp.concatenate([instr[x, :, 0].reshape(count, HD) for x in (qa, qb)], axis=0)
        v2 = with_ones(
            jnp.concatenate([instr[x, :, 1].reshape(count, HD) for x in (qa, qb)], axis=0)
        )
        for i in range(nq):
            m, acc = merge(h, i, dot_t(q_tile(h, i), k), v2)
            if last:
                pos = lax.broadcasted_iota(jnp.int32, (QT, HD), 0) + i * QT
                res = jnp.where(pos < clen_ref[0], acc[:, :HD] / acc[:, HD:], 0.0)
                out_ref[rows_of(i), pl.ds(pl.multiple_of(h * HD, HD), HD)] = res.astype(
                    jnp.bfloat16
                )
            else:
                m_ref[h, rows_of(i), :] = m
                acc_ref[h, rows_of(i), :] = acc

    mlen[...] = jnp.full((8, 128), slen_ref[0], jnp.int32)
    pl.semaphore_wait(barrier, plane - 1 + nz - 1 + 2)

    def pool_piece(h, part):
        quarter = r1.shape[3]
        return pool_ref.at[
            :,
            pl.ds(pl.multiple_of(part * quarter, quarter), quarter),
            pl.ds(pl.multiple_of(h * HD, HD), HD),
        ]

    def p1(j):
        dst = (me + j) % plane
        return rcopy(
            pool_piece(dst % nt, dst // nt), r1.at[s, t], s1.at[j], v1.at[j], plane_dev(dst)
        )

    def p1_in(j):
        src = (me + plane - j) % plane
        return rcopy(
            r1.at[0, 0], r1.at[src // nt, src % nt], s1.at[j], v1.at[j], plane_dev(src)
        )

    @pl.loop(1, plane)
    def _(j):
        p1(j).start()

    pk = rcopy(skv_ref, prev, sp.at[0], vp.at[0], nxt)
    pn = rcopy(mlen, plen, sp.at[1], vp.at[1], nxt)
    pk.start()
    pn.start()
    r1[s, t] = pool_piece(t, s)[...]

    @pl.loop(0, heads // 2)
    def _(h):
        own_part(h)

    @pl.loop(1, plane)
    def _(j):
        p1_in(j).wait_recv()

    owner = owner_ref[0]
    owner_s = owner % ns
    owner_z = owner // ns
    for b in range(nt):
        for f in range(nz // nt):
            per = x2.shape[2]
            x2[b * (nz // nt) + f] = r1[owner_s, b, :, f * per : (f + 1) * per, :]

    def p2(j):
        o = (z + ring_offset(j, nz)) % nz
        return rcopy(x2.at[o], r2.at[z], s2.at[j], v2.at[j], (o * ns + s, t))

    def p2_in(j):
        o = (z + nz - ring_offset(j, nz)) % nz
        return rcopy(x2.at[0], r2.at[o], s2.at[j], v2.at[j], (o * ns + s, t))

    @pl.loop(1, nz)
    def _(j):
        p2(nz - j).start()

    r2[z] = x2[z]
    @pl.loop(heads // 2, heads)
    def _(h):
        own_part(h)

    @pl.loop(1, nz)
    def _(j):
        p2_in(j).wait_recv()

    share = r2[owner_z]
    x3[...] = share
    instr[s, z] = share

    def p3(j):
        o = (z + ring_offset(j, nz)) % nz
        return rcopy(x3, instr.at[s, z], s3.at[j], v3.at[j], (o * ns + s, t))

    def p3_in(j):
        o = (z + nz - ring_offset(j, nz)) % nz
        return rcopy(x3, instr.at[s, o], s3.at[j], v3.at[j], (o * ns + s, t))

    @pl.loop(1, nz)
    def _(j):
        p3(nz - j).start()

    pk.wait_recv()
    pn.wait_recv()

    @pl.loop(0, heads)
    def _(h):
        prev_part(h)

    sh = ns // 2
    mate_k = (z * ns + (s // 2) * 2 + 1 - s % 2, t)
    mate_y = (z * ns + (s + sh) % ns, t)
    s_k = (s // 2) * 2 + 1 - s % 2
    s_y = (s + sh) % ns
    s_d = (s_k + sh) % ns

    def slot(j):
        return (z + nz - ring_offset(j, nz)) % nz

    def to_y(j):
        return rcopy(instr.at[s, slot(j)], instr.at[s, slot(j)], sy.at[j], vy.at[j], mate_y)

    def from_y(j):
        return rcopy(instr.at[s_y, slot(j)], instr.at[s_y, slot(j)], sy.at[j], vy.at[j], mate_y)

    def to_k(a, w, j):
        return rcopy(instr.at[a, slot(j)], instr.at[a, slot(j)], sk.at[w, j], vk.at[w, j], mate_k)

    to_y(0).start()
    to_k(s, 0, 0).start()

    @pl.loop(1, nz)
    def _(j):
        p3_in(j).wait_recv()
        to_y(j).start()
        to_k(s, 0, j).start()

    @pl.loop(0, nz)
    def _(j):
        to_k(s_k, 0, j).wait_recv()

    @pl.loop(0, heads // 2)
    def _(h):
        instr_part(h, s, s_k, False)

    @pl.loop(0, nz)
    def _(j):
        from_y(j).wait_recv()
        to_k(s_y, 1, j).start()

    @pl.loop(heads // 2, heads)
    def _(h):
        instr_part(h, s, s_k, False)

    @pl.loop(0, nz)
    def _(j):
        to_k(s_d, 1, j).wait_recv()

    @pl.loop(0, heads)
    def _(h):
        instr_part(h, s_y, s_d, True)

    @pl.loop(1, plane)
    def _(j):
        p1(j).wait_send()

    pk.wait_send()
    pn.wait_send()

    @pl.loop(1, nz)
    def _(j):
        p2(j).wait_send()
        p3(j).wait_send()

    @pl.loop(0, nz)
    def _(j):
        to_y(j).wait_send()
        to_k(s, 0, j).wait_send()
        to_k(s_y, 1, j).wait_send()


def shards(dims, queries, child_kv, summ_kv, instr_pool, child_len, summ_len, owner_group):
    nz, ns, nt = dims
    rows, width = queries.shape[1], queries.shape[2]
    heads = width // HD
    block = instr_pool.shape[1]
    summ = summ_kv.shape[2]
    quarter = block // ns
    pool = instr_pool[0].transpose(1, 0, 2)
    piece = quarter * nt // nz
    vm = pl.BlockSpec(memory_space=pltpu.VMEM)
    sm = pl.BlockSpec(memory_space=pltpu.SMEM)
    bf = jnp.bfloat16
    dma = pltpu.SemaphoreType.DMA
    out = pl.pallas_call(
        functools.partial(kernel, dims),
        name="merge_attention",
        out_shape=jax.ShapeDtypeStruct((rows, width), bf),
        in_specs=[sm, sm, vm, vm, vm, sm, vm],
        out_specs=vm,
        scratch_shapes=[
            pltpu.VMEM((ns, nt, 2, quarter, HD), bf),
            pltpu.VMEM((nz, 2, piece, HD), bf),
            pltpu.VMEM((nz, 2, piece, HD), bf),
            pltpu.VMEM((2, piece, HD), bf),
            pltpu.VMEM((ns, nz, 2, piece, HD), bf),
            pltpu.VMEM((2, summ, HD), bf),
            pltpu.VMEM((8, 128), jnp.int32),
            pltpu.VMEM((8, 128), jnp.int32),
            pltpu.VMEM((heads, rows, HD), jnp.float32),
            pltpu.VMEM((heads, rows, 2 * HD), jnp.float32),
            dma((ns * nt,)), dma((ns * nt,)),
            dma((nz,)), dma((nz,)),
            dma((nz,)), dma((nz,)),
            dma((nz,)), dma((nz,)),
            dma((2, nz)), dma((2, nz)),
            dma((2,)), dma((2,)),
        ],
        compiler_params=pltpu.CompilerParams(
            collective_id=0, has_side_effects=True, vmem_limit_bytes=56 * 1024 * 1024
        ),
    )(owner_group, child_len, queries[0], child_kv[0], summ_kv[0], summ_len, pool)
    return out[None]


def solution(mesh):
    sizes = dict(mesh.shape)
    ns = 4
    dims = (sizes["call"] // ns, ns, sizes["tensor"])
    in_specs = (
        P("call", None, "tensor"),
        P("call", None, None, "tensor"),
        P("call", None, None, "tensor"),
        P("call", "tensor", None, None),
        P("call"),
        P("call"),
        P(),
    )
    out_specs = P("call", None, "tensor")
    return jax.shard_map(
        functools.partial(shards, dims), mesh=mesh, in_specs=in_specs, out_specs=out_specs, check_vma=False
    )
```

```python
import functools
import math

import jax
import jax.numpy as jnp
from jax import lax
from jax.experimental import pallas as pl
from jax.experimental.pallas import tpu as pltpu
from jax.sharding import PartitionSpec as P

HD = 128
NEG = -1e30
LOG2E = 1.4426950408889634
MESH = pl.DeviceIdType.MESH
QT = 256


def ring_offset(j, n):
    odd = j % 2
    return odd * ((j + 1) // 2) + (1 - odd) * (n - j // 2)


def kernel(
    dims,
    owner_ref, clen_ref, q_hbm, ckv_hbm, skv_ref, slen_ref, pool_ref,
    out_ref,
    r1, x2, r2, x3, instr, prev, plen, mlen, m_ref, acc_ref, q_ref, ckv_ref,
    s1, v1, s2, v2, s3, v3, sy, vy, sk, vk, sp, vp, ld,
):
    nz, ns, nt = dims
    c = lax.axis_index("call")
    t = lax.axis_index("tensor")
    z = c // ns
    s = c % ns
    ncall = nz * ns
    plane = ns * nt
    me = s * nt + t
    heads = q_ref.shape[1] // HD
    rows = q_ref.shape[0]
    nq = rows // QT
    scale2 = LOG2E / math.sqrt(HD)

    def plane_dev(p):
        return (z * ns + p // nt, p % nt)

    def rcopy(src, dst, ssem, rsem, dev):
        return pltpu.make_async_remote_copy(
            src_ref=src, dst_ref=dst, send_sem=ssem, recv_sem=rsem,
            device_id=dev, device_id_type=MESH,
        )

    barrier = pltpu.get_barrier_semaphore()

    @pl.loop(1, plane)
    def _(j):
        pl.semaphore_signal(barrier, inc=1, device_id=plane_dev((me + j) % plane), device_id_type=MESH)

    @pl.loop(1, nz)
    def _(j):
        pl.semaphore_signal(
            barrier, inc=1, device_id=(((z + j) % nz) * ns + s, t), device_id_type=MESH
        )

    nxt = ((c + 1) % ncall, t)
    prv = ((c + ncall - 1) % ncall, t)
    pl.semaphore_signal(barrier, inc=1, device_id=nxt, device_id_type=MESH)
    pl.semaphore_signal(barrier, inc=1, device_id=prv, device_id_type=MESH)

    def dot_t(a, b):
        return lax.dot_general(a, b, (((1,), (1,)), ((), ())), preferred_element_type=jnp.float32)

    def with_ones(v):
        return jnp.concatenate([v, jnp.ones_like(v)], axis=1)

    def wide(m, n):
        return jnp.concatenate([m] * (n // HD), axis=1)

    def row_max(sc):
        return jnp.broadcast_to(jnp.max(sc, axis=1, keepdims=True), (QT, HD))

    def weights(sc, m):
        return jnp.exp2((sc - wide(m, sc.shape[1])) * scale2).astype(jnp.bfloat16)

    def rows_of(i):
        return slice(i * QT, (i + 1) * QT)

    def q_tile(h, i):
        return q_ref[rows_of(i), pl.ds(pl.multiple_of(h * HD, HD), HD)]

    def own_part(h):
        r = lax.broadcasted_iota(jnp.int32, (QT, QT), 0)
        cc = lax.broadcasted_iota(jnp.int32, (QT, QT), 1)
        scores = [dot_t(q_tile(h, i), ckv_ref[0, 0 : (i + 1) * QT, :]) for i in range(nq)]
        for i in range(nq):
            n = (i + 1) * QT
            sc = scores[i]
            diag = jnp.where(cc <= r, sc[:, n - QT : n], NEG)
            if i > 0:
                sc = jnp.concatenate([sc[:, 0 : n - QT], diag], axis=1)
            else:
                sc = diag
            m = row_max(sc)
            m_ref[h, rows_of(i), :] = m
            acc_ref[h, rows_of(i), :] = jnp.dot(
                weights(sc, m), with_ones(ckv_ref[1, 0:n, :]), preferred_element_type=jnp.float32
            )

    def merge(h, i, sc, v2):
        m0 = m_ref[h, rows_of(i), :]
        m = jnp.maximum(m0, row_max(sc))
        a = jnp.exp2((m0 - m) * scale2)
        acc = acc_ref[h, rows_of(i), :] * wide(a, 2 * HD) + jnp.dot(
            weights(sc, m), v2, preferred_element_type=jnp.float32
        )
        return m, acc

    def prev_part(h):
        count = prev.shape[1]
        ln = jnp.where(c > 0, plen[0:1, 0:1], 0)
        ok = jnp.broadcast_to(
            lax.broadcasted_iota(jnp.int32, (1, count), 1) < ln, (QT, count)
        )
        v2 = with_ones(prev[1])
        scores = [dot_t(q_tile(h, i), prev[0]) for i in range(nq)]
        for i in range(nq):
            sc = jnp.where(ok, scores[i], NEG)
            m, acc = merge(h, i, sc, v2)
            m_ref[h, rows_of(i), :] = m
            acc_ref[h, rows_of(i), :] = acc

    def instr_part(h, qa, qb, last):
        count = nz * instr.shape[3]
        k = jnp.concatenate([instr[x, :, 0].reshape(count, HD) for x in (qa, qb)], axis=0)
        v2 = with_ones(
            jnp.concatenate([instr[x, :, 1].reshape(count, HD) for x in (qa, qb)], axis=0)
        )
        scores = [dot_t(q_tile(h, i), k) for i in range(nq)]
        for i in range(nq):
            m, acc = merge(h, i, scores[i], v2)
            if last:
                pos = lax.broadcasted_iota(jnp.int32, (QT, HD), 0) + i * QT
                res = jnp.where(pos < clen_ref[0], acc[:, :HD] / acc[:, HD:], 0.0)
                out_ref[rows_of(i), pl.ds(pl.multiple_of(h * HD, HD), HD)] = res.astype(
                    jnp.bfloat16
                )
            else:
                m_ref[h, rows_of(i), :] = m
                acc_ref[h, rows_of(i), :] = acc

    load_q = pltpu.make_async_copy(q_hbm, q_ref, ld.at[0])
    load_kv = pltpu.make_async_copy(ckv_hbm, ckv_ref, ld.at[1])
    load_q.start()
    load_kv.start()
    mlen[...] = jnp.full((8, 128), slen_ref[0], jnp.int32)
    pl.semaphore_wait(barrier, plane - 1 + nz - 1 + 2)

    def pool_piece(h, part):
        quarter = r1.shape[3]
        return pool_ref.at[
            :,
            pl.ds(pl.multiple_of(part * quarter, quarter), quarter),
            pl.ds(pl.multiple_of(h * HD, HD), HD),
        ]

    def p1(j):
        dst = (me + j) % plane
        return rcopy(
            pool_piece(dst % nt, dst // nt), r1.at[s, t], s1.at[j], v1.at[j], plane_dev(dst)
        )

    def p1_in(j):
        src = (me + plane - j) % plane
        return rcopy(
            r1.at[0, 0], r1.at[src // nt, src % nt], s1.at[j], v1.at[j], plane_dev(src)
        )

    @pl.loop(1, plane)
    def _(j):
        p1(j).start()

    pk = rcopy(skv_ref, prev, sp.at[0], vp.at[0], nxt)
    pn = rcopy(mlen, plen, sp.at[1], vp.at[1], nxt)
    pk.start()
    pn.start()
    keep = pltpu.make_async_copy(pool_piece(t, s), r1.at[s, t], ld.at[2])
    keep.start()
    load_q.wait()
    load_kv.wait()

    @pl.loop(0, heads // 2)
    def _(h):
        own_part(h)

    @pl.loop(1, plane)
    def _(j):
        p1_in(j).wait_recv()

    keep.wait()
    owner = owner_ref[0]
    owner_s = owner % ns
    owner_z = owner // ns
    for b in range(nt):
        for f in range(nz // nt):
            per = x2.shape[2]
            x2[b * (nz // nt) + f] = r1[owner_s, b, :, f * per : (f + 1) * per, :]

    def p2(j):
        o = (z + ring_offset(j, nz)) % nz
        return rcopy(x2.at[o], r2.at[z], s2.at[j], v2.at[j], (o * ns + s, t))

    def p2_in(j):
        o = (z + nz - ring_offset(j, nz)) % nz
        return rcopy(x2.at[0], r2.at[o], s2.at[j], v2.at[j], (o * ns + s, t))

    @pl.loop(1, nz)
    def _(j):
        p2(nz - j).start()

    r2[z] = x2[z]
    @pl.loop(heads // 2, heads)
    def _(h):
        own_part(h)

    @pl.loop(1, nz)
    def _(j):
        p2_in(j).wait_recv()

    share = r2[owner_z]
    x3[...] = share
    instr[s, z] = share

    def p3(j):
        o = (z + ring_offset(j, nz)) % nz
        return rcopy(x3, instr.at[s, z], s3.at[j], v3.at[j], (o * ns + s, t))

    def p3_in(j):
        o = (z + nz - ring_offset(j, nz)) % nz
        return rcopy(x3, instr.at[s, o], s3.at[j], v3.at[j], (o * ns + s, t))

    @pl.loop(1, nz)
    def _(j):
        p3(nz - j).start()

    pk.wait_recv()
    pn.wait_recv()

    @pl.loop(0, heads)
    def _(h):
        prev_part(h)

    sh = ns // 2
    mate_k = (z * ns + (s // 2) * 2 + 1 - s % 2, t)
    mate_y = (z * ns + (s + sh) % ns, t)
    s_k = (s // 2) * 2 + 1 - s % 2
    s_y = (s + sh) % ns
    s_d = (s_k + sh) % ns

    def slot(j):
        return (z + nz - ring_offset(j, nz)) % nz

    def to_y(j):
        return rcopy(instr.at[s, slot(j)], instr.at[s, slot(j)], sy.at[j], vy.at[j], mate_y)

    def from_y(j):
        return rcopy(instr.at[s_y, slot(j)], instr.at[s_y, slot(j)], sy.at[j], vy.at[j], mate_y)

    def to_k(a, w, j):
        return rcopy(instr.at[a, slot(j)], instr.at[a, slot(j)], sk.at[w, j], vk.at[w, j], mate_k)

    to_y(0).start()
    to_k(s, 0, 0).start()

    @pl.loop(1, nz)
    def _(j):
        p3_in(j).wait_recv()
        to_y(j).start()
        to_k(s, 0, j).start()

    @pl.loop(0, nz)
    def _(j):
        to_k(s_k, 0, j).wait_recv()

    @pl.loop(0, heads // 2)
    def _(h):
        instr_part(h, s, s_k, False)

    @pl.loop(0, nz)
    def _(j):
        from_y(j).wait_recv()
        to_k(s_y, 1, j).start()

    @pl.loop(heads // 2, heads)
    def _(h):
        instr_part(h, s, s_k, False)

    @pl.loop(0, nz)
    def _(j):
        to_k(s_d, 1, j).wait_recv()

    @pl.loop(0, heads)
    def _(h):
        instr_part(h, s_y, s_d, True)

    @pl.loop(1, plane)
    def _(j):
        p1(j).wait_send()

    pk.wait_send()
    pn.wait_send()

    @pl.loop(1, nz)
    def _(j):
        p2(j).wait_send()
        p3(j).wait_send()

    @pl.loop(0, nz)
    def _(j):
        to_y(j).wait_send()
        to_k(s, 0, j).wait_send()
        to_k(s_y, 1, j).wait_send()


def shards(dims, queries, child_kv, summ_kv, instr_pool, child_len, summ_len, owner_group):
    nz, ns, nt = dims
    rows, width = queries.shape[1], queries.shape[2]
    heads = width // HD
    block = instr_pool.shape[1]
    summ = summ_kv.shape[2]
    quarter = block // ns
    pool = instr_pool[0].transpose(1, 0, 2)
    piece = quarter * nt // nz
    vm = pl.BlockSpec(memory_space=pltpu.VMEM)
    sm = pl.BlockSpec(memory_space=pltpu.SMEM)
    hb = pl.BlockSpec(memory_space=pl.ANY)
    bf = jnp.bfloat16
    dma = pltpu.SemaphoreType.DMA
    out = pl.pallas_call(
        functools.partial(kernel, dims),
        name="merge_attention",
        out_shape=jax.ShapeDtypeStruct((rows, width), bf),
        in_specs=[sm, sm, hb, hb, hb, sm, hb],
        out_specs=vm,
        scratch_shapes=[
            pltpu.VMEM((ns, nt, 2, quarter, HD), bf),
            pltpu.VMEM((nz, 2, piece, HD), bf),
            pltpu.VMEM((nz, 2, piece, HD), bf),
            pltpu.VMEM((2, piece, HD), bf),
            pltpu.VMEM((ns, nz, 2, piece, HD), bf),
            pltpu.VMEM((2, summ, HD), bf),
            pltpu.VMEM((8, 128), jnp.int32),
            pltpu.VMEM((8, 128), jnp.int32),
            pltpu.VMEM((heads, rows, HD), jnp.float32),
            pltpu.VMEM((heads, rows, 2 * HD), jnp.float32),
            pltpu.VMEM((rows, width), bf),
            pltpu.VMEM((2, rows, HD), bf),
            dma((ns * nt,)), dma((ns * nt,)),
            dma((nz,)), dma((nz,)),
            dma((nz,)), dma((nz,)),
            dma((nz,)), dma((nz,)),
            dma((2, nz)), dma((2, nz)),
            dma((2,)), dma((2,)),
            dma((3,)),
        ],
        compiler_params=pltpu.CompilerParams(
            collective_id=0, has_side_effects=True, vmem_limit_bytes=56 * 1024 * 1024
        ),
    )(owner_group, child_len, queries[0], child_kv[0], summ_kv[0], summ_len, pool)
    return out[None]


def solution(mesh):
    sizes = dict(mesh.shape)
    ns = 4
    dims = (sizes["call"] // ns, ns, sizes["tensor"])
    in_specs = (
        P("call", None, "tensor"),
        P("call", None, None, "tensor"),
        P("call", None, None, "tensor"),
        P("call", "tensor", None, None),
        P("call"),
        P("call"),
        P(),
    )
    out_specs = P("call", None, "tensor")
    return jax.shard_map(
        functools.partial(shards, dims), mesh=mesh, in_specs=in_specs, out_specs=out_specs, check_vma=False
    )
```
